256 devices in a mesh: pair: 32 (over y, x, core), tm: 8 (over z).
Axes of the slice: x: 4, y: 4, z: 8, core: 2. Of those that a mesh axis runs over, the one named last changes fastest.
Arguments:
- three_centre: bfloat16 [1536, 65536], P(None, 'pair'), may hold values from -0.046875 to 0.046875
- root_coulomb: bfloat16 [1536, 1536], P(('pair', 'tm')), may hold values from -0.15625 to 0.15625
- occ_depth: float32 [256], replicated, may hold values from 0.1 to 1
- vir_energy: float32 [1024], replicated, may hold values from 0.01 to 500
- occ_block: int32 [256], P('pair'), may hold values from 0 to 15
- vir_block: int32 [256], P('pair'), may hold values from 0 to 63
Outputs:
- screened: float32 [8, 1536, 1536], P('tm', 'pair')
The draws below stay inside these ranges and needn't reach their ends.
All inputs are finite; a program needn't handle non-finite values.
Results may differ from the reference program's by a relative error of at most 0.003.
Values may be sent and summed in bfloat16 or wider, within the bound.
A program may use at most 128 MiB of HBM per device.

```python
import math
import jax
import jax.numpy as jnp
from jax import lax

NAUX = 1536
OB = 16
VB = 16
NOB = 16
NVB = 64
NBLK = 256
PAIRS = 65536
TIMES = 8


def with_ends(result, own_key, least, largest):
    spot = [jax.random.randint(jax.random.fold_in(own_key, axis), (), 0, length) for axis, length in enumerate(result.shape)]
    longest = result.shape.index(max(result.shape))
    neighbour = spot[:longest] + [(spot[longest] + 1) % result.shape[longest]] + spot[longest + 1:]
    return result.at[tuple(spot)].set(least).at[tuple(neighbour)].set(largest)


def levels(key, extent, split, smallest, high):
    loudness = 1.0
    for axis_at, blocks in split:
        steps = jax.random.uniform(jax.random.fold_in(jax.random.fold_in(key, 6), axis_at), (blocks,), jnp.float32, smallest / len(split), high / len(split))
        loudness = loudness * jnp.repeat(jnp.exp(steps), extent[axis_at] // blocks).reshape((-1,) + (1,) * (len(extent) - 1 - axis_at))
    return loudness


def scatter_about(stream_key, extent, spread, limit, shards=(), kind=jnp.bfloat16):
    level = levels(stream_key, extent, shards, -0.22, 0.18) if shards else 1.0
    result = jax.random.normal(stream_key, extent, jnp.float32) * spread * level
    return jnp.minimum(jnp.maximum(result, -limit), limit).astype(kind)


def setup_inputs(seed: int = 0) -> dict:
    splits = jax.random.split(jax.random.key(seed), 7)
    return {
        "three_centre": scatter_about(splits[0], (NAUX, PAIRS), (PAIRS // 4) ** -0.5, 0.046875, ((1, 32),)),
        "root_coulomb": scatter_about(splits[1], (NAUX, NAUX), NAUX ** -0.5, 0.15625, ((0, 256),)),
        "occ_depth": jnp.clip(jnp.exp(jax.random.uniform(splits[2], (NOB * OB,), jnp.float32, math.log(0.1), math.log(1.0))), 0.1, 1.0),
        "vir_energy": jnp.clip(jnp.exp(jax.random.uniform(splits[3], (NVB * VB,), jnp.float32, math.log(0.01), math.log(500.0))), 0.01, 500.0),
        "occ_block": with_ends(jax.random.randint(splits[4], (NBLK,), 0, NOB), jax.random.fold_in(splits[4], 1), 0, NOB - 1).astype(jnp.int32),
        "vir_block": with_ends(jax.random.randint(splits[5], (NBLK,), 0, NVB), jax.random.fold_in(splits[5], 1), 0, NVB - 1).astype(jnp.int32),
    }


log_span = math.log(5000.0)


def reference(three_centre, root_coulomb, occ_depth, vir_energy, occ_block, vir_block):
    occ_sel = occ_depth.reshape(NOB, OB)[occ_block.astype(jnp.int32)]
    vir_sel = vir_energy.reshape(NVB, VB)[vir_block.astype(jnp.int32)]
    gap = (occ_sel[:, :, None] + vir_sel[:, None, :]).reshape(-1)
    whole = three_centre.astype(jnp.float32)
    steps_t = jnp.arange(TIMES).astype(jnp.float32)
    taus = 0.002 * jnp.exp(steps_t * (log_span / max(TIMES - 1, 1)))
    omegas = (steps_t + 0.5) / TIMES
    coef = 2.4 * omegas[:, None] * jnp.cos(jnp.pi * omegas[:, None] * (steps_t[None, :] + 0.5))
    decays = jnp.exp(-gap[None, :] * taus[:, None])
    freq_weight = jnp.dot(coef, decays, precision=lax.Precision.HIGHEST)
    root_whole = root_coulomb.astype(jnp.float32)
    outputs = []
    for index in range(TIMES):
        weighted = (whole * freq_weight[index][None, :]).astype(jnp.bfloat16).astype(jnp.float32)
        chi = jnp.dot(weighted, whole.T, precision=lax.Precision.HIGHEST)
        chi_low = chi.astype(jnp.bfloat16).astype(jnp.float32)
        outputs.append(jnp.dot(chi_low, root_whole, precision=lax.Precision.HIGHEST))
    return jnp.stack(outputs)
```

```python
import functools
import math

import jax
import jax.numpy as jnp
import numpy as np
from jax import lax
from jax.experimental import pallas as pl
from jax.experimental.pallas import tpu as pltpu
from jax.sharding import PartitionSpec as P

MESH = pl.DeviceIdType.MESH
NAUX = 1536
KDEV = 2048
HALF = NAUX // 2
TIMES = 8
BF = jnp.bfloat16
F32 = jnp.float32
TAUS = [0.002 * math.exp(i * (math.log(5000.0) / 7)) for i in range(TIMES)]
OMEGA = (np.arange(TIMES) + 0.5) / TIMES
COEF = (2.4 * OMEGA[:, None] * np.cos(np.pi * OMEGA[:, None] * (np.arange(TIMES)[None, :] + 0.5))).astype(np.float32)


def dot_nt(a, b):
    return lax.dot_general(a, b, (((1,), (1,)), ((), ())), preferred_element_type=F32)


def freq_weights(t, coef, occ, vir, ob, vb):
    row = lax.broadcasted_iota(jnp.int32, (8, 128), 0)
    group = lax.broadcasted_iota(jnp.int32, (8, 128), 1) // 16
    obv = jnp.zeros((8, 128), jnp.int32)
    vbv = jnp.zeros((8, 128), jnp.int32)
    for k in range(8):
        obv = jnp.where(row == k, ob[k], obv)
        vbv = jnp.where(row == k, vb[k], vbv)
    occ_sel = jnp.zeros((8, 128), F32)
    vir_sel = jnp.zeros((8, 128), F32)
    for r in range(2):
        occ_sel = jnp.where(group + 8 * r == obv, occ[r : r + 1, :], occ_sel)
    for r in range(8):
        vir_sel = jnp.where(group + 8 * r == vbv, vir[r : r + 1, :], vir_sel)
    lane_in = lax.broadcasted_iota(jnp.int32, (128, 256), 0) % 16
    lane_out = lax.broadcasted_iota(jnp.int32, (128, 256), 1)
    occ_spread = (lane_in == lane_out // 16).astype(F32)
    vir_spread = (lane_in == lane_out % 16).astype(F32)
    gap = jnp.dot(occ_sel, occ_spread, precision=lax.Precision.HIGHEST, preferred_element_type=F32)
    gap = gap + jnp.dot(vir_sel, vir_spread, precision=lax.Precision.HIGHEST, preferred_element_type=F32)
    weight = jnp.zeros((8, 256), F32)
    for i in range(TIMES):
        weight = weight + coef[t, i] * jnp.exp(-gap * np.float32(TAUS[i]))
    return weight


def kernel(
    t_hbm, root, occ, vir, ob, vb, coef, out,
    tc, wt, part, core_in, far_out, far_in, near_out, near_in, last_own, last_out, last_in, chi,
    zsend, zbuf, full,
    load_sem, core_ss, core_rs, far_ss, far_rs, near_ss, near_rs, last_ss, last_rs,
    za_ss, za_rs, b1_ss, b1_rs, b2_ss, b2_rs, sib_ss, sib_rs,
):
    p = lax.axis_index("pair")
    t = lax.axis_index("tm")
    c = lax.rem(p, 2)
    x = lax.rem(p // 2, 4)
    y = p // 8

    def dev(dx=0, dy=0, dz=0, sib=False):
        cc = 1 - c if sib else c
        xx = lax.rem(x + dx + 4, 4)
        yy = lax.rem(y + dy + 4, 4)
        zz = lax.rem(t + dz + 8, 8)
        return ((yy * 4 + xx) * 2 + cc, zz)

    pending = []

    def send(src, dst, ss, rs, device):
        copy = pltpu.make_async_remote_copy(
            src_ref=src, dst_ref=dst, send_sem=ss, recv_sem=rs, device_id=device, device_id_type=MESH
        )
        copy.start()
        pending.append(copy)
        return copy

    barrier = pltpu.get_barrier_semaphore()
    partners = [dev(sib=True)]
    partners += [dev(dx=d) for d in (1, 2, 3)] + [dev(dy=d) for d in (1, 2, 3)]
    partners += [dev(dz=d) for d in range(1, 8)]
    for partner in partners:
        pl.semaphore_signal(barrier, inc=1, device_id=partner, device_id_type=MESH)

    loads = []
    for i in range(8):
        rows = pl.ds(192 * i, 192)
        copy = pltpu.make_async_copy(t_hbm.at[rows], tc.at[rows], load_sem.at[i])
        copy.start()
        loads.append(copy)

    zsend[...] = jnp.zeros_like(zsend)
    zsend[0:6, :] = root[...]
    weight = freq_weights(t, coef, occ, vir, ob, vb)
    pl.semaphore_wait(barrier, len(partners))

    z_copies = [
        send(zsend, zbuf.at[t], za_ss.at[d - 1], za_rs.at[d - 1], dev(dz=d)) for d in range(1, 8)
    ]
    zbuf[t] = zsend[...]

    for i in range(8):
        loads[i].wait()

        def scale(j, carry):
            rows = pl.ds(pl.multiple_of(192 * i + 48 * j, 16), 48)
            for k in range(8):
                cols = slice(256 * k, 256 * k + 256)
                wt[rows, cols] = (tc[rows, cols].astype(F32) * weight[k : k + 1, :]).astype(BF)
            return carry

        lax.fori_loop(0, 4, scale, 0)

    axis = [x, y]

    def place(h, g):
        return lax.rem(axis[h] + (2, 1, 3, 0)[g], 4)

    def along(h, d):
        return dev(dx=d) if h == 0 else dev(dy=d)

    core_copies = {}
    others = pl.ds(pl.multiple_of(48 * (1 - c), 16), 48)
    ours = pl.ds(pl.multiple_of(48 * c, 16), 48)

    def gemm(g, h):
        pos = place(h, g)
        lhs = []
        for j in range(4):
            chip = 4 * j + pos if h == 0 else 4 * pos + j
            lhs.append(wt[pl.ds(pl.multiple_of(96 * chip, 32), 96), :])
        res = dot_nt(jnp.concatenate(lhs, axis=0), tc[HALF * h : HALF * h + HALF, :])
        n = 2 * g + h
        for j in range(4):
            part[n, j] = res[96 * j : 96 * j + 96, :].astype(BF)
        core_copies[n] = send(
            part.at[n, :, others, :], core_in.at[n], core_ss.at[n], core_rs.at[n], dev(sib=True)
        )

    def pair_sum(n, j):
        return part[n, j, ours, :].astype(F32) + core_in[n, j].astype(F32)

    far_copies, near_copies, last_copies = {}, {}, {}

    def far(h):
        n = h
        core_copies[n].wait_recv()
        for j in range(4):
            far_out[h, j] = pair_sum(n, j).astype(BF)
        for s, d in ((0, 1), (1, 3)):
            far_copies[h, s] = send(
                far_out.at[h, pl.ds(2 * s, 2)], far_in.at[h, s], far_ss.at[h, s], far_rs.at[h, s], along(h, d)
            )

    def near(h, s, late):
        n = 2 * (1 + s) + h
        if not late:
            core_copies[n].wait_recv()
        else:
            far_copies[h, s].wait_recv()
        first = 2 * s if late else 2 - 2 * s
        for i in range(2):
            total = pair_sum(n, first + i)
            if late:
                total = total + far_in[h, s, i].astype(F32)
            near_out[h, s, first + i] = total.astype(BF)
        block = pl.ds(first, 2)
        near_copies[h, s, late] = send(
            near_out.at[h, s, block],
            near_in.at[h, s, block],
            near_ss.at[h, s, int(late)],
            near_rs.at[h, s, int(late)],
            along(h, 1 if s == 0 else 3),
        )

    def last(h):
        n = 6 + h
        core_copies[n].wait_recv()
        for s in range(2):
            for late in (False, True):
                near_copies[h, s, late].wait_recv()
        for j in range(4):
            total = pair_sum(n, j) + near_in[h, 0, j].astype(F32) + near_in[h, 1, j].astype(F32)
            last_own[h, j] = total
            last_out[h, j] = total.astype(BF)
        for d in range(1, 4):
            j = lax.rem(axis[1 - h] + d, 4)
            last_copies[h, d] = send(
                last_out.at[h, j], last_in.at[h, d - 1], last_ss.at[h, d - 1], last_rs.at[h, d - 1], along(1 - h, d)
            )

    def finish(h):
        total = last_own[h, axis[1 - h]]
        for d in range(1, 4):
            last_copies[h, d].wait_recv()
            total = total + last_in[h, d - 1].astype(F32)
        chi[:, HALF * h : HALF * h + HALF] = total.astype(BF)

    def first(d):
        return lax.rem(x + d * (1 - c), 4), lax.rem(y + d * c, 4)

    def second(i):
        return x * c + i * (1 - c), y * (1 - c) + i * c

    def dev_at(xx, yy):
        return ((yy * 4 + xx) * 2 + c, t)

    b1, b2, sib = [], {}, []

    def to_sibling(xx, yy):
        block = full.at[4 * yy + xx, c]
        k = len(sib)
        sib.append(send(block, block, sib_ss.at[k], sib_rs.at[k], dev(sib=True)))

    def root_first():
        for copy in z_copies:
            copy.wait_recv()
        i = lax.broadcasted_iota(jnp.int32, (48, 64), 0)
        r = lax.broadcasted_iota(jnp.int32, (48, 64), 1)
        rows8 = jnp.concatenate([zbuf[k].astype(F32) for k in range(8)], axis=0).astype(BF)
        pick = ((r // 8 == i // 6) & (r % 8 == i % 6)).astype(BF)
        full[4 * y + x, c] = jnp.dot(pick, rows8, preferred_element_type=F32).astype(BF)
        block = full.at[4 * y + x, c]
        for d in range(1, 4):
            b1.append(send(block, block, b1_ss.at[d - 1], b1_rs.at[d - 1], dev_at(*first(d))))

    def root_second():
        for copy in b1:
            copy.wait_recv()
        for d in range(1, 4):
            to = dev_at(lax.rem(x + d * c, 4), lax.rem(y + d * (1 - c), 4))
            for i in range(4):
                xx, yy = second(i)
                block = full.at[4 * yy + xx, c]
                b2[d, i] = send(block, block, b2_ss.at[d - 1, i], b2_rs.at[d - 1, i], to)
        for i in range(4):
            to_sibling(*second(i))

    def root_third():
        for d in range(1, 4):
            for i in range(4):
                b2[d, i].wait_recv()
                xx, yy = second(i)
                to_sibling(lax.rem(xx + (4 - d) * c, 4), lax.rem(yy + (4 - d) * (1 - c), 4))

    gemm(0, 0)
    gemm(0, 1)
    far(0)
    gemm(1, 0)
    far(1)
    gemm(1, 1)
    near(0, 0, False)
    root_first()
    gemm(2, 0)
    near(1, 0, False)
    near(0, 1, False)
    gemm(2, 1)
    near(1, 1, False)
    near(0, 0, True)
    near(0, 1, True)
    root_second()
    gemm(3, 0)
    near(1, 0, True)
    near(1, 1, True)
    gemm(3, 1)
    last(0)
    last(1)
    root_third()
    finish(0)
    finish(1)
    for copy in sib:
        copy.wait_recv()
    out[0] = jnp.dot(chi[...], full[...].reshape(NAUX, NAUX), preferred_element_type=F32)
    for copy in pending:
        copy.wait_send()


def shards(three_centre, root_coulomb, occ_depth, vir_energy, occ_block, vir_block):
    dma = pltpu.SemaphoreType.DMA
    vmem = pl.BlockSpec(memory_space=pltpu.VMEM)
    smem = pl.BlockSpec(memory_space=pltpu.SMEM)
    return pl.pallas_call(
        kernel,
        out_shape=jax.ShapeDtypeStruct((1, 48, NAUX), F32),
        in_specs=[pl.BlockSpec(memory_space=pl.ANY), vmem, vmem, vmem, smem, smem, smem],
        out_specs=vmem,
        scratch_shapes=[
            pltpu.VMEM((NAUX, KDEV), BF),
            pltpu.VMEM((NAUX, KDEV), BF),
            pltpu.VMEM((8, 4, 96, HALF), BF),
            pltpu.VMEM((8, 4, 48, HALF), BF),
            pltpu.VMEM((2, 4, 48, HALF), BF),
            pltpu.VMEM((2, 2, 2, 48, HALF), BF),
            pltpu.VMEM((2, 2, 4, 48, HALF), BF),
            pltpu.VMEM((2, 2, 4, 48, HALF), BF),
            pltpu.VMEM((2, 4, 48, HALF), F32),
            pltpu.VMEM((2, 4, 48, HALF), BF),
            pltpu.VMEM((2, 3, 48, HALF), BF),
            pltpu.VMEM((48, NAUX), BF),
            pltpu.VMEM((8, NAUX), BF),
            pltpu.VMEM((8, 8, NAUX), BF),
            pltpu.VMEM((16, 2, 48, NAUX), BF),
            dma((8,)), dma((8,)), dma((8,)), dma((2, 2)), dma((2, 2)), dma((2, 2, 2)), dma((2, 2, 2)),
            dma((2, 3)), dma((2, 3)),
            dma((7,)), dma((7,)), dma((3,)), dma((3,)), dma((3, 4)), dma((3, 4)), dma((16,)), dma((16,)),
        ],
        compiler_params=pltpu.CompilerParams(
            collective_id=0, has_side_effects=True, vmem_limit_bytes=60 * 1024 * 1024
        ),
    )(
        three_centre,
        root_coulomb,
        occ_depth.reshape(2, 128),
        vir_energy.reshape(8, 128),
        occ_block,
        vir_block,
        jnp.asarray(COEF),
    )


def solution(mesh):
    in_specs = (P(None, "pair"), P(("pair", "tm"), None), P(), P(), P("pair"), P("pair"))
    out_specs = P("tm", "pair", None)
    return jax.shard_map(shards, mesh=mesh, in_specs=in_specs, out_specs=out_specs, check_vma=False)
```

```python
import functools
import math

import jax
import jax.numpy as jnp
import numpy as np
from jax import lax
from jax.experimental import pallas as pl
from jax.experimental.pallas import tpu as pltpu
from jax.sharding import PartitionSpec as P

MESH = pl.DeviceIdType.MESH
NAUX = 1536
KDEV = 2048
HALF = NAUX // 2
TIMES = 8
BF = jnp.bfloat16
F32 = jnp.float32
TAUS = [0.002 * math.exp(i * (math.log(5000.0) / 7)) for i in range(TIMES)]
OMEGA = (np.arange(TIMES) + 0.5) / TIMES
COEF = (2.4 * OMEGA[:, None] * np.cos(np.pi * OMEGA[:, None] * (np.arange(TIMES)[None, :] + 0.5))).astype(np.float32)


def dot_nt(a, b):
    return lax.dot_general(a, b, (((1,), (1,)), ((), ())), preferred_element_type=F32)


def freq_weights(t, coef, occ, vir, ob, vb):
    row = lax.broadcasted_iota(jnp.int32, (8, 128), 0)
    group = lax.broadcasted_iota(jnp.int32, (8, 128), 1) // 16
    obv = jnp.zeros((8, 128), jnp.int32)
    vbv = jnp.zeros((8, 128), jnp.int32)
    for k in range(8):
        obv = jnp.where(row == k, ob[k], obv)
        vbv = jnp.where(row == k, vb[k], vbv)
    occ_sel = jnp.zeros((8, 128), F32)
    vir_sel = jnp.zeros((8, 128), F32)
    for r in range(2):
        occ_sel = jnp.where(group + 8 * r == obv, occ[r : r + 1, :], occ_sel)
    for r in range(8):
        vir_sel = jnp.where(group + 8 * r == vbv, vir[r : r + 1, :], vir_sel)
    lane_in = lax.broadcasted_iota(jnp.int32, (128, 256), 0) % 16
    lane_out = lax.broadcasted_iota(jnp.int32, (128, 256), 1)
    occ_spread = (lane_in == lane_out // 16).astype(F32)
    vir_spread = (lane_in == lane_out % 16).astype(F32)
    gap = jnp.dot(occ_sel, occ_spread, precision=lax.Precision.HIGHEST, preferred_element_type=F32)
    gap = gap + jnp.dot(vir_sel, vir_spread, precision=lax.Precision.HIGHEST, preferred_element_type=F32)
    weight = jnp.zeros((8, 256), F32)
    for i in range(TIMES):
        weight = weight + coef[t, i] * jnp.exp(-gap * np.float32(TAUS[i]))
    return weight


def kernel(
    t_hbm, root, occ, vir, ob, vb, coef, out,
    tc, wt, part, core_in, far_out, far_in, near_out, near_in, last_own, last_out, last_in, chi,
    zsend, zbuf, full,
    load_sem, core_ss, core_rs, far_ss, far_rs, near_ss, near_rs, last_ss, last_rs,
    za_ss, za_rs, root_ss, root_rs, half_ss, half_rs, sib_ss, sib_rs,
):
    p = lax.axis_index("pair")
    t = lax.axis_index("tm")
    c = lax.rem(p, 2)
    x = lax.rem(p // 2, 4)
    y = p // 8

    def dev(dx=0, dy=0, dz=0, sib=False):
        cc = 1 - c if sib else c
        xx = lax.rem(x + dx + 4, 4)
        yy = lax.rem(y + dy + 4, 4)
        zz = lax.rem(t + dz + 8, 8)
        return ((yy * 4 + xx) * 2 + cc, zz)

    pending = []

    def send(src, dst, ss, rs, device):
        copy = pltpu.make_async_remote_copy(
            src_ref=src, dst_ref=dst, send_sem=ss, recv_sem=rs, device_id=device, device_id_type=MESH
        )
        copy.start()
        pending.append(copy)
        return copy

    barrier = pltpu.get_barrier_semaphore()
    partners = [dev(sib=True)]
    partners += [dev(dx=d) for d in (1, 2, 3)] + [dev(dy=d) for d in (1, 2, 3)]
    partners += [dev(dz=d) for d in range(1, 8)]
    for partner in partners:
        pl.semaphore_signal(barrier, inc=1, device_id=partner, device_id_type=MESH)

    loads = []
    for i in range(8):
        rows = pl.ds(192 * i, 192)
        copy = pltpu.make_async_copy(t_hbm.at[rows], tc.at[rows], load_sem.at[i])
        copy.start()
        loads.append(copy)

    zsend[...] = jnp.zeros_like(zsend)
    zsend[0:6, :] = root[...]
    weight = freq_weights(t, coef, occ, vir, ob, vb)

    for i in range(8):
        loads[i].wait()

        def scale(j, carry):
            rows = pl.ds(pl.multiple_of(192 * i + 48 * j, 16), 48)
            for k in range(8):
                cols = slice(256 * k, 256 * k + 256)
                wt[rows, cols] = (tc[rows, cols].astype(F32) * weight[k : k + 1, :]).astype(BF)
            return carry

        lax.fori_loop(0, 4, scale, 0)

    axis = [x, y]

    def place(h, g):
        return lax.rem(axis[h] + (2, 1, 3, 0)[g], 4)

    def along(h, d):
        return dev(dx=d) if h == 0 else dev(dy=d)

    core_copies = {}

    def gemm(g, h):
        pos = place(h, g)
        lhs = []
        for j in range(4):
            chip = 4 * j + pos if h == 0 else 4 * pos + j
            lhs.append(wt[pl.ds(pl.multiple_of(96 * chip, 32), 96), :])
        res = dot_nt(jnp.concatenate(lhs, axis=0), tc[HALF * h : HALF * h + HALF, :])
        n = 2 * g + h
        for j in range(4):
            for s in range(2):
                part[n, s, j] = res[96 * j + 48 * s : 96 * j + 48 * s + 48, :].astype(BF)

    def swap(g, h):
        n = 2 * g + h
        core_copies[n] = send(
            part.at[n, 1 - c], core_in.at[n], core_ss.at[n], core_rs.at[n], dev(sib=True)
        )

    def pair_sum(n, j):
        return part[n, c, j].astype(F32) + core_in[n, j].astype(F32)

    far_copies, near_copies, last_copies = {}, {}, {}

    def far(h):
        n = h
        core_copies[n].wait_recv()
        for j in range(4):
            far_out[h, j] = pair_sum(n, j).astype(BF)
        for s, d in ((0, 1), (1, 3)):
            far_copies[h, s] = send(
                far_out.at[h, pl.ds(2 * s, 2)], far_in.at[h, s], far_ss.at[h, s], far_rs.at[h, s], along(h, d)
            )

    def near(h, s, late):
        n = 2 * (1 + s) + h
        if not late:
            core_copies[n].wait_recv()
        else:
            far_copies[h, s].wait_recv()
        first = 2 * s if late else 2 - 2 * s
        for i in range(2):
            total = pair_sum(n, first + i)
            if late:
                total = total + far_in[h, s, i].astype(F32)
            near_out[h, s, first + i] = total.astype(BF)
        block = pl.ds(first, 2)
        near_copies[h, s, late] = send(
            near_out.at[h, s, block],
            near_in.at[h, s, block],
            near_ss.at[h, s, int(late)],
            near_rs.at[h, s, int(late)],
            along(h, 1 if s == 0 else 3),
        )

    def last(h):
        n = 6 + h
        core_copies[n].wait_recv()
        for s in range(2):
            for late in (False, True):
                near_copies[h, s, late].wait_recv()
        for j in range(4):
            total = pair_sum(n, j) + near_in[h, 0, j].astype(F32) + near_in[h, 1, j].astype(F32)
            last_own[h, j] = total
            last_out[h, j] = total.astype(BF)
        for d in range(1, 4):
            j = lax.rem(axis[1 - h] + d, 4)
            last_copies[h, d] = send(
                last_out.at[h, j], last_in.at[h, d - 1], last_ss.at[h, d - 1], last_rs.at[h, d - 1], along(1 - h, d)
            )

    def finish(h):
        total = last_own[h, axis[1 - h]]
        for d in range(1, 4):
            last_copies[h, d].wait_recv()
            total = total + last_in[h, d - 1].astype(F32)
        chi[:, HALF * h : HALF * h + HALF] = total.astype(BF)

    def chip_at(a, b):
        xx = lax.rem(x + a * (1 - c) + b * c, 4)
        yy = lax.rem(y + a * c + b * (1 - c), 4)
        return 4 * yy + xx

    def slot(a, b):
        return full.at[chip_at(a, b), c]

    def first(d):
        return (2 * chip_at(d, 0) + c, t)

    def second(d):
        return (2 * chip_at(0, d) + c, t)

    got = {}
    sib = []

    def pass_on(a, b, to, a2, b2):
        got[a2, b2] = send(slot(a, b), slot(a, b), root_ss.at[a2, b2], root_rs.at[a2, b2], to)

    def to_sibling(a, b):
        k = len(sib)
        sib.append(send(slot(a, b), slot(a, b), sib_ss.at[k], sib_rs.at[k], dev(sib=True)))

    def to_seconds(a):
        pass_on(a, 0, second(1), a, 3)
        pass_on(a, 0, second(3), a, 1)

    def root_own():
        for copy in z_copies:
            copy.wait_recv()
        i = lax.broadcasted_iota(jnp.int32, (48, 64), 0)
        r = lax.broadcasted_iota(jnp.int32, (48, 64), 1)
        rows8 = jnp.concatenate([zbuf[k].astype(F32) for k in range(8)], axis=0).astype(BF)
        pick = ((r // 8 == i // 6) & (r % 8 == i % 6)).astype(BF)
        full[4 * y + x, c] = jnp.dot(pick, rows8, preferred_element_type=F32).astype(BF)
        pass_on(0, 0, first(1), 3, 0)
        pass_on(0, 0, first(3), 1, 0)
        to_seconds(0)
        to_sibling(0, 0)

    halves = {}

    def root_near():
        for k, (a, to) in enumerate(((3, 1), (1, 3))):
            got[a, 0].wait_recv()
            part_cols = full.at[chip_at(a, 0), c, :, pl.ds(HALF * k, HALF)]
            halves[k] = send(part_cols, part_cols, half_ss.at[k], half_rs.at[k], first(to))
            to_seconds(a)
            to_sibling(a, 0)

    def root_far():
        for k in range(2):
            halves[k].wait_recv()
        to_seconds(2)
        to_sibling(2, 0)

    def root_turn(a):
        for b in (3, 1):
            got[a, b].wait_recv()
            if (b == 3) == (a in (0, 3)):
                pass_on(a, b, second(4 - b), a, 2)
            to_sibling(a, b)

    def root_end(a):
        got[a, 2].wait_recv()
        to_sibling(a, 2)

    pl.semaphore_wait(barrier, len(partners))
    z_copies = [
        send(zsend, zbuf.at[t], za_ss.at[d - 1], za_rs.at[d - 1], dev(dz=d)) for d in range(1, 8)
    ]
    zbuf[t] = zsend[...]
    gemm(0, 0)
    swap(0, 0)
    gemm(0, 1)
    swap(0, 1)
    far(0)
    gemm(1, 0)
    swap(1, 0)
    far(1)
    gemm(1, 1)
    swap(1, 1)
    near(0, 0, False)
    root_own()
    gemm(2, 0)
    swap(2, 0)
    near(1, 0, False)
    near(0, 1, False)
    gemm(2, 1)
    swap(2, 1)
    near(1, 1, False)
    near(0, 0, True)
    near(0, 1, True)
    root_near()
    gemm(3, 0)
    swap(3, 0)
    near(1, 0, True)
    near(1, 1, True)
    gemm(3, 1)
    swap(3, 1)
    root_far()
    root_turn(0)
    last(0)
    root_turn(3)
    last(1)
    root_turn(1)
    root_turn(2)
    root_end(0)
    root_end(3)
    root_end(1)
    root_end(2)
    finish(0)
    finish(1)
    for copy in sib:
        copy.wait_recv()
    out[0] = jnp.dot(chi[...], full[...].reshape(NAUX, NAUX), preferred_element_type=F32)
    for copy in pending:
        copy.wait_send()


def shards(three_centre, root_coulomb, occ_depth, vir_energy, occ_block, vir_block):
    dma = pltpu.SemaphoreType.DMA
    vmem = pl.BlockSpec(memory_space=pltpu.VMEM)
    smem = pl.BlockSpec(memory_space=pltpu.SMEM)
    return pl.pallas_call(
        kernel,
        out_shape=jax.ShapeDtypeStruct((1, 48, NAUX), F32),
        in_specs=[pl.BlockSpec(memory_space=pl.ANY), vmem, vmem, vmem, smem, smem, smem],
        out_specs=vmem,
        scratch_shapes=[
            pltpu.VMEM((NAUX, KDEV), BF),
            pltpu.VMEM((NAUX, KDEV), BF),
            pltpu.VMEM((8, 2, 4, 48, HALF), BF),
            pltpu.VMEM((8, 4, 48, HALF), BF),
            pltpu.VMEM((2, 4, 48, HALF), BF),
            pltpu.VMEM((2, 2, 2, 48, HALF), BF),
            pltpu.VMEM((2, 2, 4, 48, HALF), BF),
            pltpu.VMEM((2, 2, 4, 48, HALF), BF),
            pltpu.VMEM((2, 4, 48, HALF), F32),
            pltpu.VMEM((2, 4, 48, HALF), BF),
            pltpu.VMEM((2, 3, 48, HALF), BF),
            pltpu.VMEM((48, NAUX), BF),
            pltpu.VMEM((8, NAUX), BF),
            pltpu.VMEM((8, 8, NAUX), BF),
            pltpu.VMEM((16, 2, 48, NAUX), BF),
            dma((8,)), dma((8,)), dma((8,)), dma((2, 2)), dma((2, 2)), dma((2, 2, 2)), dma((2, 2, 2)),
            dma((2, 3)), dma((2, 3)),
            dma((7,)), dma((7,)), dma((4, 4)), dma((4, 4)), dma((2,)), dma((2,)), dma((16,)), dma((16,)),
        ],
        compiler_params=pltpu.CompilerParams(
            collective_id=0, has_side_effects=True, vmem_limit_bytes=60 * 1024 * 1024
        ),
    )(
        three_centre,
        root_coulomb,
        occ_depth.reshape(2, 128),
        vir_energy.reshape(8, 128),
        occ_block,
        vir_block,
        jnp.asarray(COEF),
    )


def solution(mesh):
    in_specs = (P(None, "pair"), P(("pair", "tm"), None), P(), P(), P("pair"), P("pair"))
    out_specs = P("tm", "pair", None)
    return jax.shard_map(shards, mesh=mesh, in_specs=in_specs, out_specs=out_specs, check_vma=False)
```

```python
import functools
import math

import jax
import jax.numpy as jnp
import numpy as np
from jax import lax
from jax.experimental import pallas as pl
from jax.experimental.pallas import tpu as pltpu
from jax.sharding import PartitionSpec as P

MESH = pl.DeviceIdType.MESH
NAUX = 1536
KDEV = 2048
HALF = NAUX // 2
TIMES = 8
BF = jnp.bfloat16
F32 = jnp.float32
TAUS = [0.002 * math.exp(i * (math.log(5000.0) / 7)) for i in range(TIMES)]
OMEGA = (np.arange(TIMES) + 0.5) / TIMES
ORDER = np.arange(HALF).reshape(8, 2, TIMES, 6).transpose(1, 2, 0, 3).reshape(-1)
REORDER = (np.arange(HALF)[:, None] == ORDER[None, :]).astype(np.float32)
COEF = (2.4 * OMEGA[:, None] * np.cos(np.pi * OMEGA[:, None] * (np.arange(TIMES)[None, :] + 0.5))).astype(np.float32)


def dot_nt(a, b):
    return lax.dot_general(a, b, (((1,), (1,)), ((), ())), preferred_element_type=F32)


def freq_weights(t, coef, occ, vir, ob, vb):
    row = lax.broadcasted_iota(jnp.int32, (8, 128), 0)
    group = lax.broadcasted_iota(jnp.int32, (8, 128), 1) // 16
    obv = jnp.zeros((8, 128), jnp.int32)
    vbv = jnp.zeros((8, 128), jnp.int32)
    for k in range(8):
        obv = jnp.where(row == k, ob[k], obv)
        vbv = jnp.where(row == k, vb[k], vbv)
    occ_sel = jnp.zeros((8, 128), F32)
    vir_sel = jnp.zeros((8, 128), F32)
    for r in range(2):
        occ_sel = jnp.where(group + 8 * r == obv, occ[r : r + 1, :], occ_sel)
    for r in range(8):
        vir_sel = jnp.where(group + 8 * r == vbv, vir[r : r + 1, :], vir_sel)
    lane_in = lax.broadcasted_iota(jnp.int32, (128, 256), 0) % 16
    lane_out = lax.broadcasted_iota(jnp.int32, (128, 256), 1)
    occ_spread = (lane_in == lane_out // 16).astype(F32)
    vir_spread = (lane_in == lane_out % 16).astype(F32)
    gap = jnp.dot(occ_sel, occ_spread, precision=lax.Precision.HIGHEST, preferred_element_type=F32)
    gap = gap + jnp.dot(vir_sel, vir_spread, precision=lax.Precision.HIGHEST, preferred_element_type=F32)
    weight = jnp.zeros((8, 256), F32)
    for i in range(TIMES):
        weight = weight + coef[t, i] * jnp.exp(-gap * np.float32(TAUS[i]))
    return weight


def kernel(
    t_hbm, root, occ, vir, ob, vb, coef, reorder_hbm, out,
    tc, wt, part, core_in, far_out, far_in, near_out, near_in, last_own, last_out, last_in, chi,
    zsend, zbuf, full, plane, zr, reorder, chi_perm,
    load_sem, core_ss, core_rs, far_ss, far_rs, near_ss, near_rs, last_ss, last_rs,
    za_ss, za_rs, root_ss, root_rs, half_ss, half_rs, sib_ss, sib_rs,
    plane_ss, plane_rs, zr_ss, zr_rs, reorder_sem,
):
    p = lax.axis_index("pair")
    t = lax.axis_index("tm")
    c = lax.rem(p, 2)
    x = lax.rem(p // 2, 4)
    y = p // 8

    def dev(dx=0, dy=0, dz=0, sib=False):
        cc = 1 - c if sib else c
        xx = lax.rem(x + dx + 4, 4)
        yy = lax.rem(y + dy + 4, 4)
        zz = lax.rem(t + dz + 8, 8)
        return ((yy * 4 + xx) * 2 + cc, zz)

    pending = []

    def send(src, dst, ss, rs, device):
        copy = pltpu.make_async_remote_copy(
            src_ref=src, dst_ref=dst, send_sem=ss, recv_sem=rs, device_id=device, device_id_type=MESH
        )
        copy.start()
        pending.append(copy)
        return copy

    barrier = pltpu.get_barrier_semaphore()
    partners = [dev(sib=True)]
    partners += [dev(dx=d) for d in (1, 2, 3)] + [dev(dy=d) for d in (1, 2, 3)]
    partners += [dev(dx=i, dy=j) for i in (1, 2, 3) for j in (1, 2, 3)]
    partners += [dev(dz=d) for d in range(1, 8)]
    for partner in partners:
        pl.semaphore_signal(barrier, inc=1, device_id=partner, device_id_type=MESH)

    loads = []
    for i in range(8):
        rows = pl.ds(192 * i, 192)
        copy = pltpu.make_async_copy(t_hbm.at[rows], tc.at[rows], load_sem.at[i])
        copy.start()
        loads.append(copy)

    reorder_copy = pltpu.make_async_copy(reorder_hbm, reorder, reorder_sem)
    reorder_copy.start()
    zsend[...] = jnp.zeros_like(zsend)
    zsend[0:6, :] = root[...]
    weight = freq_weights(t, coef, occ, vir, ob, vb)

    for i in range(8):
        loads[i].wait()

        def scale(j, carry):
            rows = pl.ds(pl.multiple_of(192 * i + 48 * j, 16), 48)
            for k in range(8):
                cols = slice(256 * k, 256 * k + 256)
                wt[rows, cols] = (tc[rows, cols].astype(F32) * weight[k : k + 1, :]).astype(BF)
            return carry

        lax.fori_loop(0, 4, scale, 0)

    axis = [x, y]

    def place(h, g):
        return lax.rem(axis[h] + (2, 1, 3, 0)[g], 4)

    def along(h, d):
        return dev(dx=d) if h == 0 else dev(dy=d)

    core_copies = {}

    def gemm(g, h):
        pos = place(h, g)
        lhs = []
        for j in range(4):
            chip = 4 * j + pos if h == 0 else 4 * pos + j
            lhs.append(wt[pl.ds(pl.multiple_of(96 * chip, 32), 96), :])
        res = dot_nt(jnp.concatenate(lhs, axis=0), tc[HALF * h : HALF * h + HALF, :])
        n = 2 * g + h
        for j in range(4):
            for s in range(2):
                part[n, s, j] = res[96 * j + 48 * s : 96 * j + 48 * s + 48, :].astype(BF)

    def swap(g, h):
        n = 2 * g + h
        core_copies[n] = send(
            part.at[n, 1 - c], core_in.at[n], core_ss.at[n], core_rs.at[n], dev(sib=True)
        )

    def pair_sum(n, j):
        return part[n, c, j].astype(F32) + core_in[n, j].astype(F32)

    far_copies, near_copies, last_copies = {}, {}, {}

    def far(h):
        n = h
        core_copies[n].wait_recv()
        for j in range(4):
            far_out[h, j] = pair_sum(n, j).astype(BF)
        for s, d in ((0, 1), (1, 3)):
            far_copies[h, s] = send(
                far_out.at[h, pl.ds(2 * s, 2)], far_in.at[h, s], far_ss.at[h, s], far_rs.at[h, s], along(h, d)
            )

    def near(h, s, late):
        n = 2 * (1 + s) + h
        if not late:
            core_copies[n].wait_recv()
        else:
            far_copies[h, s].wait_recv()
        first = 2 * s if late else 2 - 2 * s
        for i in range(2):
            total = pair_sum(n, first + i)
            if late:
                total = total + far_in[h, s, i].astype(F32)
            near_out[h, s, first + i] = total.astype(BF)
        block = pl.ds(first, 2)
        near_copies[h, s, late] = send(
            near_out.at[h, s, block],
            near_in.at[h, s, block],
            near_ss.at[h, s, int(late)],
            near_rs.at[h, s, int(late)],
            along(h, 1 if s == 0 else 3),
        )

    def last(h):
        n = 6 + h
        core_copies[n].wait_recv()
        for s in range(2):
            for late in (False, True):
                near_copies[h, s, late].wait_recv()
        for j in range(4):
            total = pair_sum(n, j) + near_in[h, 0, j].astype(F32) + near_in[h, 1, j].astype(F32)
            last_own[h, j] = total
            last_out[h, j] = total.astype(BF)
        for d in range(1, 4):
            j = lax.rem(axis[1 - h] + d, 4)
            last_copies[h, d] = send(
                last_out.at[h, j], last_in.at[h, d - 1], last_ss.at[h, d - 1], last_rs.at[h, d - 1], along(1 - h, d)
            )

    def finish(h):
        total = last_own[h, axis[1 - h]]
        for d in range(1, 4):
            last_copies[h, d].wait_recv()
            total = total + last_in[h, d - 1].astype(F32)
        chi[:, HALF * h : HALF * h + HALF] = total.astype(BF)

    def chip_at(a, b):
        xx = lax.rem(x + a * (1 - c) + b * c, 4)
        yy = lax.rem(y + a * c + b * (1 - c), 4)
        return 4 * yy + xx

    def slot(a, b):
        return full.at[chip_at(a, b), c]

    def first(d):
        return (2 * chip_at(d, 0) + c, t)

    def second(d):
        return (2 * chip_at(0, d) + c, t)

    got = {}
    sib = []

    def pass_on(a, b, to, a2, b2):
        got[a2, b2] = send(slot(a, b), slot(a, b), root_ss.at[a2, b2], root_rs.at[a2, b2], to)

    def share(block):
        k = len(sib)
        sib.append(send(block, block, sib_ss.at[k], sib_rs.at[k], dev(sib=True)))

    def to_sibling(a, b):
        share(slot(a, b))

    def compact(blocks):
        i = lax.broadcasted_iota(jnp.int32, (48, 64), 0)
        r = lax.broadcasted_iota(jnp.int32, (48, 64), 1)
        rows8 = jnp.concatenate([block.astype(F32) for block in blocks], axis=0).astype(BF)
        pick = ((r // 8 == i // 6) & (r % 8 == i % 6)).astype(BF)
        return jnp.dot(pick, rows8, preferred_element_type=F32).astype(BF)

    ring = {}

    def ring_send(k, s, g):
        source = lax.rem(t + (1 - s if k == 0 else s - 1) + 8, 8)
        block = zr.at[c, source, g]
        ring[k, s, g] = send(
            block, block, zr_ss.at[k, s - 1, g], zr_rs.at[k, s - 1, g], dev(dz=1 if k == 0 else -1)
        )

    def plane_own():
        for copy in plane_copies:
            copy.wait_recv()
        for g in range(2):
            zr[c, t, g] = compact([plane[8 * g + i] for i in range(8)])
            for k in range(2):
                ring_send(k, 1, g)
        for g in range(2):
            share(zr.at[c, t, g])

    def ring_step(s):
        for g in range(2):
            for k in range(2):
                if s == 4 and g != k:
                    continue
                ring[k, s, g].wait_recv()
                if s < 3 or (s == 3 and g == k):
                    ring_send(k, s + 1, g)
                share(zr.at[c, lax.rem(t + (8 - s if k == 0 else s), 8), g])

    def to_seconds(a):
        pass_on(a, 0, second(1), a, 3)
        pass_on(a, 0, second(3), a, 1)

    def root_own():
        for copy in z_copies:
            copy.wait_recv()
        full[4 * y + x, c] = compact([zbuf[k] for k in range(8)])
        pass_on(0, 0, first(1), 3, 0)
        pass_on(0, 0, first(3), 1, 0)
        to_seconds(0)
        to_sibling(0, 0)

    halves = {}

    def root_near():
        for k, (a, to) in enumerate(((3, 1), (1, 3))):
            got[a, 0].wait_recv()
            part_cols = full.at[chip_at(a, 0), c, :, pl.ds(HALF // 2 * k, HALF // 2)]
            halves[k] = send(part_cols, part_cols, half_ss.at[k], half_rs.at[k], first(to))
            to_seconds(a)
            to_sibling(a, 0)

    def root_far():
        for k in range(2):
            halves[k].wait_recv()
        to_seconds(2)
        to_sibling(2, 0)

    def root_turn(a):
        for b in (3, 1):
            got[a, b].wait_recv()
            if (b == 3) == (a in (0, 3)):
                pass_on(a, b, second(4 - b), a, 2)
            to_sibling(a, b)

    def root_end(a):
        got[a, 2].wait_recv()
        to_sibling(a, 2)

    pl.semaphore_wait(barrier, len(partners))
    z_copies = [
        send(zsend.at[:, pl.ds(0, HALF)], zbuf.at[t], za_ss.at[d - 1], za_rs.at[d - 1], dev(dz=d)) for d in range(1, 8)
    ]
    zbuf[t] = zsend[:, 0:HALF]
    plane_copies = [
        send(
            zsend.at[:, pl.ds(HALF, HALF)], plane.at[4 * y + x], plane_ss.at[i, j], plane_rs.at[i, j], dev(dx=i, dy=j)
        )
        for i in range(4)
        for j in range(4)
        if i or j
    ]
    plane[4 * y + x] = zsend[:, HALF:NAUX]
    gemm(0, 0)
    swap(0, 0)
    gemm(0, 1)
    swap(0, 1)
    far(0)
    gemm(1, 0)
    swap(1, 0)
    far(1)
    gemm(1, 1)
    swap(1, 1)
    near(0, 0, False)
    root_own()
    plane_own()
    gemm(2, 0)
    swap(2, 0)
    near(1, 0, False)
    near(0, 1, False)
    gemm(2, 1)
    swap(2, 1)
    near(1, 1, False)
    ring_step(1)
    near(0, 0, True)
    near(0, 1, True)
    root_near()
    gemm(3, 0)
    swap(3, 0)
    near(1, 0, True)
    near(1, 1, True)
    ring_step(2)
    gemm(3, 1)
    swap(3, 1)
    root_far()
    root_turn(0)
    last(0)
    ring_step(3)
    root_turn(3)
    last(1)
    root_turn(1)
    root_turn(2)
    ring_step(4)
    root_end(0)
    root_end(3)
    root_end(1)
    root_end(2)
    reorder_copy.wait()
    for h in range(2):
        finish(h)
        half = jnp.dot(chi[:, HALF * h : HALF * h + HALF], reorder[...], preferred_element_type=F32)
        chi_perm[:, HALF * h : HALF * h + HALF] = half.astype(BF)
    for copy in sib:
        copy.wait_recv()
    out[0, :, 0:HALF] = jnp.dot(chi[...], full[...].reshape(NAUX, HALF), preferred_element_type=F32)
    planes = [
        jnp.dot(chi_perm[:, HALF * g : HALF * g + HALF], zr[:, :, g].reshape(HALF, HALF), preferred_element_type=F32)
        for g in range(2)
    ]
    out[0, :, HALF:NAUX] = planes[0] + planes[1]
    for copy in pending:
        copy.wait_send()


def shards(three_centre, root_coulomb, occ_depth, vir_energy, occ_block, vir_block):
    dma = pltpu.SemaphoreType.DMA
    vmem = pl.BlockSpec(memory_space=pltpu.VMEM)
    smem = pl.BlockSpec(memory_space=pltpu.SMEM)
    return pl.pallas_call(
        kernel,
        out_shape=jax.ShapeDtypeStruct((1, 48, NAUX), F32),
        in_specs=[pl.BlockSpec(memory_space=pl.ANY), vmem, vmem, vmem, smem, smem, smem, pl.BlockSpec(memory_space=pl.ANY)],
        out_specs=vmem,
        scratch_shapes=[
            pltpu.VMEM((NAUX, KDEV), BF),
            pltpu.VMEM((NAUX, KDEV), BF),
            pltpu.VMEM((8, 2, 4, 48, HALF), BF),
            pltpu.VMEM((8, 4, 48, HALF), BF),
            pltpu.VMEM((2, 4, 48, HALF), BF),
            pltpu.VMEM((2, 2, 2, 48, HALF), BF),
            pltpu.VMEM((2, 2, 4, 48, HALF), BF),
            pltpu.VMEM((2, 2, 4, 48, HALF), BF),
            pltpu.VMEM((2, 4, 48, HALF), F32),
            pltpu.VMEM((2, 4, 48, HALF), BF),
            pltpu.VMEM((2, 3, 48, HALF), BF),
            pltpu.VMEM((48, NAUX), BF),
            pltpu.VMEM((8, NAUX), BF),
            pltpu.VMEM((8, 8, HALF), BF),
            pltpu.VMEM((16, 2, 48, HALF), BF),
            pltpu.VMEM((16, 8, HALF), BF),
            pltpu.VMEM((2, TIMES, 2, 48, HALF), BF),
            pltpu.VMEM((HALF, HALF), BF),
            pltpu.VMEM((48, NAUX), BF),
            dma((8,)), dma((8,)), dma((8,)), dma((2, 2)), dma((2, 2)), dma((2, 2, 2)), dma((2, 2, 2)),
            dma((2, 3)), dma((2, 3)),
            dma((7,)), dma((7,)), dma((4, 4)), dma((4, 4)), dma((2,)), dma((2,)), dma((32,)), dma((32,)),
            dma((4, 4)), dma((4, 4)), dma((2, 4, 2)), dma((2, 4, 2)), dma,
        ],
        compiler_params=pltpu.CompilerParams(
            collective_id=0, has_side_effects=True, vmem_limit_bytes=60 * 1024 * 1024
        ),
    )(
        three_centre,
        root_coulomb,
        occ_depth.reshape(2, 128),
        vir_energy.reshape(8, 128),
        occ_block,
        vir_block,
        jnp.asarray(COEF),
        jnp.asarray(REORDER, BF),
    )


def solution(mesh):
    in_specs = (P(None, "pair"), P(("pair", "tm"), None), P(), P(), P("pair"), P("pair"))
    out_specs = P("tm", "pair", None)
    return jax.shard_map(shards, mesh=mesh, in_specs=in_specs, out_specs=out_specs, check_vma=False)
```

```python
import functools
import math

import jax
import jax.numpy as jnp
import numpy as np
from jax import lax
from jax.experimental import pallas as pl
from jax.experimental.pallas import tpu as pltpu
from jax.sharding import PartitionSpec as P

MESH = pl.DeviceIdType.MESH
NAUX = 1536
KDEV = 2048
HALF = NAUX // 2
TIMES = 8
BF = jnp.bfloat16
F32 = jnp.float32
TAUS = [0.002 * math.exp(i * (math.log(5000.0) / 7)) for i in range(TIMES)]
OMEGA = (np.arange(TIMES) + 0.5) / TIMES
ORDER = np.arange(HALF).reshape(8, 2, TIMES, 6).transpose(1, 2, 0, 3).reshape(-1)
REORDER = (np.arange(HALF)[:, None] == ORDER[None, :]).astype(np.float32)
COEF = (2.4 * OMEGA[:, None] * np.cos(np.pi * OMEGA[:, None] * (np.arange(TIMES)[None, :] + 0.5))).astype(np.float32)


def dot_nt(a, b):
    return lax.dot_general(a, b, (((1,), (1,)), ((), ())), preferred_element_type=F32)


def freq_weights(t, coef, occ, vir, ob, vb):
    row = lax.broadcasted_iota(jnp.int32, (8, 128), 0)
    group = lax.broadcasted_iota(jnp.int32, (8, 128), 1) // 16
    obv = jnp.zeros((8, 128), jnp.int32)
    vbv = jnp.zeros((8, 128), jnp.int32)
    for k in range(8):
        obv = jnp.where(row == k, ob[k], obv)
        vbv = jnp.where(row == k, vb[k], vbv)
    occ_sel = jnp.zeros((8, 128), F32)
    vir_sel = jnp.zeros((8, 128), F32)
    for r in range(2):
        occ_sel = jnp.where(group + 8 * r == obv, occ[r : r + 1, :], occ_sel)
    for r in range(8):
        vir_sel = jnp.where(group + 8 * r == vbv, vir[r : r + 1, :], vir_sel)
    lane_in = lax.broadcasted_iota(jnp.int32, (128, 256), 0) % 16
    lane_out = lax.broadcasted_iota(jnp.int32, (128, 256), 1)
    occ_spread = (lane_in == lane_out // 16).astype(F32)
    vir_spread = (lane_in == lane_out % 16).astype(F32)
    gap = jnp.dot(occ_sel, occ_spread, precision=lax.Precision.HIGHEST, preferred_element_type=F32)
    gap = gap + jnp.dot(vir_sel, vir_spread, precision=lax.Precision.HIGHEST, preferred_element_type=F32)
    weight = jnp.zeros((8, 256), F32)
    for i in range(TIMES):
        weight = weight + coef[t, i] * jnp.exp(-gap * np.float32(TAUS[i]))
    return weight


def kernel(
    t_hbm, root, occ, vir, ob, vb, coef, reorder_hbm, out,
    tc, wt, part, core_in, far_out, far_in, near_out, near_in, last_own, last_out, last_in, chi,
    zsend, zbuf, full, plane, zr, reorder, chi_perm,
    load_sem, core_ss, core_rs, far_ss, far_rs, near_ss, near_rs, last_ss, last_rs,
    za_ss, za_rs, root_ss, root_rs, half_ss, half_rs, sib_ss, sib_rs,
    plane_ss, plane_rs, zr_ss, zr_rs, reorder_sem,
):
    p = lax.axis_index("pair")
    t = lax.axis_index("tm")
    c = lax.rem(p, 2)
    x = lax.rem(p // 2, 4)
    y = p // 8

    def dev(dx=0, dy=0, dz=0, sib=False):
        cc = 1 - c if sib else c
        xx = lax.rem(x + dx + 4, 4)
        yy = lax.rem(y + dy + 4, 4)
        zz = lax.rem(t + dz + 8, 8)
        return ((yy * 4 + xx) * 2 + cc, zz)

    pending = []

    def send(src, dst, ss, rs, device):
        copy = pltpu.make_async_remote_copy(
            src_ref=src, dst_ref=dst, send_sem=ss, recv_sem=rs, device_id=device, device_id_type=MESH
        )
        copy.start()
        pending.append(copy)
        return copy

    barrier = pltpu.get_barrier_semaphore()
    partners = [dev(sib=True)]
    partners += [dev(dx=d) for d in (1, 2, 3)] + [dev(dy=d) for d in (1, 2, 3)]
    partners += [dev(dx=i, dy=j) for i in (1, 2, 3) for j in (1, 2, 3)]
    partners += [dev(dz=d) for d in range(1, 8)]
    for partner in partners:
        pl.semaphore_signal(barrier, inc=1, device_id=partner, device_id_type=MESH)

    loads = []
    for i in range(8):
        rows = pl.ds(192 * i, 192)
        copy = pltpu.make_async_copy(t_hbm.at[rows], tc.at[rows], load_sem.at[i])
        copy.start()
        loads.append(copy)

    reorder_copy = pltpu.make_async_copy(reorder_hbm, reorder, reorder_sem)
    reorder_copy.start()
    zsend[...] = jnp.zeros_like(zsend)
    zsend[0:6, :] = root[...]
    weight = freq_weights(t, coef, occ, vir, ob, vb)

    for i in range(8):
        loads[i].wait()

        def scale(j, carry):
            rows = pl.ds(pl.multiple_of(192 * i + 48 * j, 16), 48)
            for k in range(8):
                cols = slice(256 * k, 256 * k + 256)
                wt[rows, cols] = (tc[rows, cols].astype(F32) * weight[k : k + 1, :]).astype(BF)
            return carry

        lax.fori_loop(0, 4, scale, 0)

    axis = [x, y]

    def place(h, g):
        return lax.rem(axis[h] + (2, 1, 3, 0)[g], 4)

    def along(h, d):
        return dev(dx=d) if h == 0 else dev(dy=d)

    core_copies = {}

    def gemm(g, h):
        pos = place(h, g)
        lhs = []
        for j in range(4):
            chip = 4 * j + pos if h == 0 else 4 * pos + j
            lhs.append(wt[pl.ds(pl.multiple_of(96 * chip, 32), 96), :])
        res = dot_nt(jnp.concatenate(lhs, axis=0), tc[HALF * h : HALF * h + HALF, :])
        n = 2 * g + h
        for j in range(4):
            for s in range(2):
                part[n, s, j] = res[96 * j + 48 * s : 96 * j + 48 * s + 48, :].astype(BF)

    def swap(g, h):
        n = 2 * g + h
        core_copies[n] = send(
            part.at[n, 1 - c], core_in.at[n], core_ss.at[n], core_rs.at[n], dev(sib=True)
        )

    def pair_sum(n, j):
        return part[n, c, j].astype(F32) + core_in[n, j].astype(F32)

    far_copies, near_copies, last_copies = {}, {}, {}

    def far(h):
        n = h
        core_copies[n].wait_recv()
        for j in range(4):
            far_out[h, j] = pair_sum(n, j).astype(BF)
        for s, d in ((0, 1), (1, 3)):
            far_copies[h, s] = send(
                far_out.at[h, pl.ds(2 * s, 2)], far_in.at[h, s], far_ss.at[h, s], far_rs.at[h, s], along(h, d)
            )

    def near(h, s, late):
        n = 2 * (1 + s) + h
        if not late:
            core_copies[n].wait_recv()
        else:
            far_copies[h, s].wait_recv()
        first = 2 * s if late else 2 - 2 * s
        for i in range(2):
            total = pair_sum(n, first + i)
            if late:
                total = total + far_in[h, s, i].astype(F32)
            near_out[h, s, first + i] = total.astype(BF)
        block = pl.ds(first, 2)
        near_copies[h, s, late] = send(
            near_out.at[h, s, block],
            near_in.at[h, s, block],
            near_ss.at[h, s, int(late)],
            near_rs.at[h, s, int(late)],
            along(h, 1 if s == 0 else 3),
        )

    def last(h):
        n = 6 + h
        core_copies[n].wait_recv()
        for s in range(2):
            for late in (False, True):
                near_copies[h, s, late].wait_recv()
        for j in range(4):
            total = pair_sum(n, j) + near_in[h, 0, j].astype(F32) + near_in[h, 1, j].astype(F32)
            last_own[h, j] = total
            last_out[h, j] = total.astype(BF)
        for d in range(1, 4):
            j = lax.rem(axis[1 - h] + d, 4)
            last_copies[h, d] = send(
                last_out.at[h, j], last_in.at[h, d - 1], last_ss.at[h, d - 1], last_rs.at[h, d - 1], along(1 - h, d)
            )

    def finish(h):
        total = last_own[h, axis[1 - h]]
        for d in range(1, 4):
            last_copies[h, d].wait_recv()
            total = total + last_in[h, d - 1].astype(F32)
        chi[:, HALF * h : HALF * h + HALF] = total.astype(BF)

    def finish_reordered(h):
        finish(h)
        half = jnp.dot(chi[:, HALF * h : HALF * h + HALF], reorder[...], preferred_element_type=F32)
        chi_perm[:, HALF * h : HALF * h + HALF] = half.astype(BF)

    def chip_at(a, b):
        xx = lax.rem(x + a * (1 - c) + b * c, 4)
        yy = lax.rem(y + a * c + b * (1 - c), 4)
        return 4 * yy + xx

    def slot(a, b):
        return full.at[chip_at(a, b), c]

    def first(d):
        return (2 * chip_at(d, 0) + c, t)

    def second(d):
        return (2 * chip_at(0, d) + c, t)

    got = {}
    sib = []

    def pass_on(a, b, to, a2, b2):
        got[a2, b2] = send(slot(a, b), slot(a, b), root_ss.at[a2, b2], root_rs.at[a2, b2], to)

    def share(block):
        k = len(sib)
        sib.append(send(block, block, sib_ss.at[k], sib_rs.at[k], dev(sib=True)))

    def to_sibling(a, b):
        share(slot(a, b))

    def compact(blocks):
        i = lax.broadcasted_iota(jnp.int32, (48, 64), 0)
        r = lax.broadcasted_iota(jnp.int32, (48, 64), 1)
        rows8 = jnp.concatenate([block.astype(F32) for block in blocks], axis=0).astype(BF)
        pick = ((r // 8 == i // 6) & (r % 8 == i % 6)).astype(BF)
        return jnp.dot(pick, rows8, preferred_element_type=F32).astype(BF)

    ring = {}

    def ring_send(k, s, g):
        source = lax.rem(t + (1 - s if k == 0 else s - 1) + 8, 8)
        block = zr.at[c, source, g]
        ring[k, s, g] = send(
            block, block, zr_ss.at[k, s - 1, g], zr_rs.at[k, s - 1, g], dev(dz=1 if k == 0 else -1)
        )

    def plane_own():
        for copy in plane_copies:
            copy.wait_recv()
        for g in range(2):
            zr[c, t, g] = compact([plane[8 * g + i] for i in range(8)])
            for k in range(2):
                ring_send(k, 1, g)
        for g in range(2):
            share(zr.at[c, t, g])

    def ring_step(s):
        for g in range(2):
            for k in range(2):
                if s == 4 and g != k:
                    continue
                ring[k, s, g].wait_recv()
                if s < 3 or (s == 3 and g == k):
                    ring_send(k, s + 1, g)
                share(zr.at[c, lax.rem(t + (8 - s if k == 0 else s), 8), g])

    def to_seconds(a):
        pass_on(a, 0, second(1), a, 3)
        pass_on(a, 0, second(3), a, 1)

    def root_own():
        for copy in z_copies:
            copy.wait_recv()
        full[4 * y + x, c] = compact([zbuf[k] for k in range(8)])
        pass_on(0, 0, first(1), 3, 0)
        pass_on(0, 0, first(3), 1, 0)
        to_seconds(0)
        to_sibling(0, 0)

    halves = {}

    def root_near():
        for k, (a, to) in enumerate(((3, 1), (1, 3))):
            got[a, 0].wait_recv()
            part_cols = full.at[chip_at(a, 0), c, :, pl.ds(HALF // 2 * k, HALF // 2)]
            halves[k] = send(part_cols, part_cols, half_ss.at[k], half_rs.at[k], first(to))
            to_seconds(a)
            to_sibling(a, 0)

    def root_far():
        for k in range(2):
            halves[k].wait_recv()
        to_seconds(2)
        to_sibling(2, 0)

    def root_turn(a):
        for b in (3, 1):
            got[a, b].wait_recv()
            if (b == 3) == (a in (0, 3)):
                pass_on(a, b, second(4 - b), a, 2)
            to_sibling(a, b)

    def root_end(a):
        got[a, 2].wait_recv()
        to_sibling(a, 2)

    pl.semaphore_wait(barrier, len(partners))
    z_copies = [
        send(zsend.at[:, pl.ds(0, HALF)], zbuf.at[t], za_ss.at[d - 1], za_rs.at[d - 1], dev(dz=d)) for d in range(1, 8)
    ]
    zbuf[t] = zsend[:, 0:HALF]
    plane_copies = [
        send(
            zsend.at[:, pl.ds(HALF, HALF)], plane.at[4 * y + x], plane_ss.at[i, j], plane_rs.at[i, j], dev(dx=i, dy=j)
        )
        for i in range(4)
        for j in range(4)
        if i or j
    ]
    plane[4 * y + x] = zsend[:, HALF:NAUX]
    gemm(0, 0)
    swap(0, 0)
    gemm(0, 1)
    swap(0, 1)
    far(0)
    gemm(1, 0)
    swap(1, 0)
    far(1)
    gemm(1, 1)
    swap(1, 1)
    near(0, 0, False)
    root_own()
    plane_own()
    gemm(2, 0)
    swap(2, 0)
    near(1, 0, False)
    near(0, 1, False)
    gemm(2, 1)
    swap(2, 1)
    near(1, 1, False)
    ring_step(1)
    near(0, 0, True)
    near(0, 1, True)
    root_near()
    gemm(3, 0)
    swap(3, 0)
    near(1, 0, True)
    near(1, 1, True)
    ring_step(2)
    gemm(3, 1)
    swap(3, 1)
    root_far()
    root_turn(0)
    last(0)
    ring_step(3)
    root_turn(3)
    last(1)
    root_turn(1)
    root_turn(2)
    ring_step(4)
    reorder_copy.wait()
    finish_reordered(0)
    root_end(0)
    root_end(3)
    root_end(1)
    root_end(2)
    finish_reordered(1)
    for copy in sib:
        copy.wait_recv()
    out[0, :, 0:HALF] = jnp.dot(chi[...], full[...].reshape(NAUX, HALF), preferred_element_type=F32)
    planes = [
        jnp.dot(chi_perm[:, HALF * g : HALF * g + HALF], zr[:, :, g].reshape(HALF, HALF), preferred_element_type=F32)
        for g in range(2)
    ]
    out[0, :, HALF:NAUX] = planes[0] + planes[1]
    for copy in pending:
        copy.wait_send()


def shards(three_centre, root_coulomb, occ_depth, vir_energy, occ_block, vir_block):
    dma = pltpu.SemaphoreType.DMA
    vmem = pl.BlockSpec(memory_space=pltpu.VMEM)
    smem = pl.BlockSpec(memory_space=pltpu.SMEM)
    return pl.pallas_call(
        kernel,
        out_shape=jax.ShapeDtypeStruct((1, 48, NAUX), F32),
        in_specs=[pl.BlockSpec(memory_space=pl.ANY), vmem, vmem, vmem, smem, smem, smem, pl.BlockSpec(memory_space=pl.ANY)],
        out_specs=vmem,
        scratch_shapes=[
            pltpu.VMEM((NAUX, KDEV), BF),
            pltpu.VMEM((NAUX, KDEV), BF),
            pltpu.VMEM((8, 2, 4, 48, HALF), BF),
            pltpu.VMEM((8, 4, 48, HALF), BF),
            pltpu.VMEM((2, 4, 48, HALF), BF),
            pltpu.VMEM((2, 2, 2, 48, HALF), BF),
            pltpu.VMEM((2, 2, 4, 48, HALF), BF),
            pltpu.VMEM((2, 2, 4, 48, HALF), BF),
            pltpu.VMEM((2, 4, 48, HALF), F32),
            pltpu.VMEM((2, 4, 48, HALF), BF),
            pltpu.VMEM((2, 3, 48, HALF), BF),
            pltpu.VMEM((48, NAUX), BF),
            pltpu.VMEM((8, NAUX), BF),
            pltpu.VMEM((8, 8, HALF), BF),
            pltpu.VMEM((16, 2, 48, HALF), BF),
            pltpu.VMEM((16, 8, HALF), BF),
            pltpu.VMEM((2, TIMES, 2, 48, HALF), BF),
            pltpu.VMEM((HALF, HALF), BF),
            pltpu.VMEM((48, NAUX), BF),
            dma((8,)), dma((8,)), dma((8,)), dma((2, 2)), dma((2, 2)), dma((2, 2, 2)), dma((2, 2, 2)),
            dma((2, 3)), dma((2, 3)),
            dma((7,)), dma((7,)), dma((4, 4)), dma((4, 4)), dma((2,)), dma((2,)), dma((32,)), dma((32,)),
            dma((4, 4)), dma((4, 4)), dma((2, 4, 2)), dma((2, 4, 2)), dma,
        ],
        compiler_params=pltpu.CompilerParams(
            collective_id=0, has_side_effects=True, vmem_limit_bytes=60 * 1024 * 1024
        ),
    )(
        three_centre,
        root_coulomb,
        occ_depth.reshape(2, 128),
        vir_energy.reshape(8, 128),
        occ_block,
        vir_block,
        jnp.asarray(COEF),
        jnp.asarray(REORDER, BF),
    )


def solution(mesh):
    in_specs = (P(None, "pair"), P(("pair", "tm"), None), P(), P(), P("pair"), P("pair"))
    out_specs = P("tm", "pair", None)
    return jax.shard_map(shards, mesh=mesh, in_specs=in_specs, out_specs=out_specs, check_vma=False)
```
